32 devices in a mesh: dp: 8 (over z, y), mp: 4 (over x, core).
Axes of the slice: x: 2, y: 2, z: 4, core: 2. Of those that a mesh axis runs over, the one named last changes fastest.
Arguments:
- token_pool: bfloat16 [4096, 3072], P('dp'), may hold values from -6 to 6
- visible: int32 [1024], P('dp'), may hold values from 0 to 511, as said below
- out_grad: bfloat16 [1024, 3072], P('dp'), may hold values from -2.5 to 2.5
- ln_gain: float32 [3072], replicated, may hold values from 0.5 to 1.5
- master_up: float32 [3072, 12288], P('dp', 'mp'), may hold values from -0.109375 to 0.109375
- master_down: float32 [3072, 12288], P('dp', 'mp'), may hold values from -0.0546875 to 0.0546875
- row_up: float32 [3072], P('dp'), may hold values from 0.02 to 5
- col_up: float32 [12288], P('mp'), may hold values from 0.05 to 0.5
- row_down: float32 [3072], P('dp'), may hold values from 0.02 to 5
- col_down: float32 [12288], P('mp'), may hold values from 0.05 to 0.5
Outputs:
- update_up: float32 [3072, 12288], P('dp', 'mp')
- update_down: float32 [3072, 12288], P('dp', 'mp')
- row_up_new: float32 [3072], P('dp')
- col_up_new: float32 [12288], P('mp')
- row_down_new: float32 [3072], P('dp')
- col_down_new: float32 [12288], P('mp')
The draws below stay inside these ranges and needn't reach their ends.
Inputs may be any that keep to these rules, and one draw needn't show every extreme that they name: `visible`: each aligned block of 128 entries lists distinct patch indices of that block's 512 patches, in rising order.
All inputs are finite; a program needn't handle non-finite values.
Results may differ from the reference program's by a relative error of at most 0.0059.
Values may be sent and summed in bfloat16 or wider, within the bound.
A program may use at most 256 MiB of HBM per device.

```python
import math
import jax
import jax.numpy as jnp
from jax import lax

D = 3072
FF = 12288
TOK_DEV = 128
ALL_DEV = 512
TOKENS = 1024
POOL = 4096


def draw_visible(key, part):
    blocks = TOKENS // TOK_DEV
    keys = jax.random.split(jax.random.fold_in(key, 17), blocks)
    orders = jax.vmap(lambda one_key: jax.random.permutation(one_key, ALL_DEV))(keys)
    chosen = jnp.sort(orders[:, :TOK_DEV], axis=1)
    return chosen.reshape(-1).astype(jnp.int32)


def rising_factor(key, salt):
    place = jnp.arange(D, dtype=jnp.float32) / max(D - 1, 1)
    jitter = jnp.exp(jax.random.uniform(jax.random.fold_in(key, salt), (D,), jnp.float32, -0.35, 0.35))
    base = 0.05 * jnp.exp(place * jnp.log(40.0))
    return (base * jitter).astype(jnp.float32)


def draw_row_up(key, part):
    return rising_factor(key, 31)


def draw_row_down(key, part):
    return rising_factor(key, 47)


def strengthened(array, rng, source, target, parts, factor):
    def block_of(dim):
        return (jnp.arange(array.shape[dim]) // (array.shape[dim] // parts)).reshape((-1,) + (1,) * (array.ndim - 1 - dim))

    one_side = jax.random.permutation(rng, parts)[block_of(target)]
    far = (block_of(target) + parts // 2) % parts
    return jnp.where((block_of(source) == one_side) | (block_of(source) == far), factor * array, array)


def shard_levels(rng, dims, pieces, least, largest):
    def one(axis_at, parts):
        heights = jax.random.uniform(jax.random.fold_in(jax.random.fold_in(rng, 6), axis_at), (parts,), jnp.float32, least / len(pieces), largest / len(pieces))
        return jnp.repeat(jnp.exp(heights), dims[axis_at] // parts).reshape((-1,) + (1,) * (len(dims) - axis_at - 1))

    level = one(*pieces[0])
    for cut in pieces[1:]:
        level = level * one(*cut)
    return level


def bell_draw(own_key, dims, width, reach, shards=(), kind=jnp.bfloat16):
    array = jax.random.normal(own_key, dims, jnp.float32) * width
    if len(shards) > 0:
        array = shard_levels(own_key, dims, shards, -0.22, 0.18) * array
    return jnp.clip(array, min=-reach, max=reach).astype(kind)


def noise_with(key, shape, deviation, reach, cuts, heavy, kind=jnp.bfloat16):
    entries = deviation * jax.random.normal(key, shape, jnp.float32)
    if cuts:
        entries = entries * shard_levels(key, shape, cuts, -0.22, 0.18)
    return jnp.clip(strengthened(entries, jax.random.fold_in(key, 3), *heavy), -reach, reach).astype(kind)


def setup_inputs(seed: int = 0) -> dict:
    arg_keys = jax.random.split(jax.random.key(seed), 11)
    token_pool = noise_with(arg_keys[0], (POOL, D), 1.0, 6.0, ((0, 8),), (0, 1, 8, 2.0))
    visible = draw_visible(jax.random.fold_in(arg_keys[10], 71), 0)
    out_grad = noise_with(arg_keys[2], (TOKENS, D), (4.0 * TOKENS ** -0.5), 2.5, ((0, 8),), (0, 1, 8, 2.0))
    ln_gain = jnp.clip(1.0 + 0.1 * jax.random.normal(arg_keys[3], (D,), jnp.float32), 0.5, 1.5)
    master_up = bell_draw(arg_keys[4], (D, FF), D ** -0.5, 0.109375, ((0, 8), (1, 4)), jnp.float32)
    master_down = bell_draw(arg_keys[5], (D, FF), FF ** -0.5, 0.0546875, ((0, 8), (1, 4)), jnp.float32)
    row_up = draw_row_up(jax.random.fold_in(arg_keys[10], 71), 0)
    col_up = jnp.clip(jnp.exp(math.log(0.5) - 2.3025851 * jax.random.uniform(arg_keys[7], (FF,), jnp.float32) ** shard_levels(arg_keys[7], (FF,), ((0, 4),), -0.2, 0.2)), 0.05, 0.5)
    row_down = draw_row_down(jax.random.fold_in(arg_keys[10], 71), 0)
    col_down = jnp.clip(jnp.exp(math.log(0.5) - 2.3025851 * jax.random.uniform(arg_keys[9], (FF,), jnp.float32) ** shard_levels(arg_keys[9], (FF,), ((0, 4),), -0.2, 0.2)), 0.05, 0.5)
    return {"token_pool": token_pool, "visible": visible, "out_grad": out_grad, "ln_gain": ln_gain, "master_up": master_up, "master_down": master_down, "row_up": row_up, "col_up": col_up, "row_down": row_down, "col_down": col_down}


decay_rate = 0.8
norm_eps = 1e-06
tiny_value = 1e-30

def gelu_tanh(values):
    return jax.nn.gelu(values, approximate=True)

def normalize(values, gain):
    mean_val = lax.optimization_barrier(jnp.mean(values, axis=1, keepdims=True))
    centred = values - mean_val
    variance = lax.optimization_barrier(jnp.mean(centred * centred, axis=1, keepdims=True))
    return (centred * lax.rsqrt(variance + norm_eps) * gain).astype(jnp.bfloat16)

def contract_tokens(left, right):
    return lax.dot_general(left, right, (((0,), (0,)), ((), ())), preferred_element_type=jnp.float32)

def factored_update(grad, row_old, col_old):
    squares = grad * grad + tiny_value
    row_new = decay_rate * row_old + (1.0 - decay_rate) * lax.optimization_barrier(jnp.mean(squares, axis=1))
    col_new = decay_rate * col_old + (1.0 - decay_rate) * lax.optimization_barrier(jnp.mean(squares, axis=0))
    raw = grad * lax.rsqrt(row_new[:, None] * col_new[None, :])
    spread = jnp.sqrt(jnp.mean(raw * raw))
    return (raw / jnp.maximum(1.0, spread), row_new, col_new)

def reference(token_pool, visible, out_grad, ln_gain, master_up, master_down, row_up, col_up, row_down, col_down):
    owner = jnp.arange(visible.shape[0], dtype=jnp.int32) // TOK_DEV * ALL_DEV
    picked = token_pool[(visible + owner).astype(jnp.int32)].astype(jnp.float32)
    normed = normalize(picked, ln_gain)
    w_up = master_up.astype(jnp.bfloat16)
    w_down = master_down.astype(jnp.bfloat16)
    pre_act = jnp.dot(normed, w_up, preferred_element_type=jnp.float32)
    act_value, pull_back = jax.vjp(gelu_tanh, pre_act)
    hidden_act = act_value.astype(jnp.bfloat16)
    act_grad = jnp.dot(out_grad, w_down, preferred_element_type=jnp.float32)
    pre_grad = pull_back(act_grad)[0].astype(jnp.bfloat16)
    grad_up = contract_tokens(normed, pre_grad)
    grad_down = contract_tokens(out_grad, hidden_act)
    update_up, row_up_new, col_up_new = factored_update(grad_up, row_up, col_up)
    update_down, row_down_new, col_down_new = factored_update(grad_down, row_down, col_down)
    return (update_up, update_down, row_up_new, col_up_new, row_down_new, col_down_new)
```

```python
import functools
import jax
import jax.numpy as jnp
from jax import lax
from jax.experimental import pallas as pl
from jax.experimental.pallas import tpu as pltpu
from jax.sharding import PartitionSpec as P

decay_rate = 0.8
norm_eps = 1e-06
tiny_value = 1e-30


def gelu_tanh(values):
    return jax.nn.gelu(values, approximate=True)


def normalize(values, gain):
    mean_val = jnp.mean(values, axis=1, keepdims=True)
    centred = values - mean_val
    variance = jnp.mean(centred * centred, axis=1, keepdims=True)
    return (centred * lax.rsqrt(variance + norm_eps) * gain).astype(jnp.bfloat16)


def contract_tokens(left, right):
    return lax.dot_general(
        left, right, (((0,), (0,)), ((), ())), preferred_element_type=jnp.float32
    )


def finish_update(grad, row_new, col_new):
    return grad * lax.rsqrt(row_new[:, None] * col_new[None, :])


def gathered_grads(normed, out_grad, w_up, w_down):
    left = normed
    pre_act = jnp.dot(
        left, lax.all_gather(w_up, "dp", axis=0, tiled=True), preferred_element_type=jnp.float32
    )
    act_value, pull_back = jax.vjp(gelu_tanh, pre_act)
    hidden_act = act_value.astype(jnp.bfloat16)
    left = out_grad
    act_grad = jnp.dot(
        left, lax.all_gather(w_down, "dp", axis=0, tiled=True), preferred_element_type=jnp.float32
    )
    pre_grad = pull_back(act_grad)[0].astype(jnp.bfloat16)
    grad_down = lax.psum_scatter(
        contract_tokens(out_grad, hidden_act), "dp", scatter_dimension=0, tiled=True
    )
    grad_up = lax.psum_scatter(
        contract_tokens(normed, pre_grad), "dp", scatter_dimension=0, tiled=True
    )
    return grad_up, grad_down


MESH = pl.DeviceIdType.MESH


def flipped(index):
    return index + 1 - 2 * lax.rem(index, 2)


def greet(devices):
    barrier = pltpu.get_barrier_semaphore()
    for device in devices:
        pl.semaphore_signal(barrier, inc=1, device_id=device, device_id_type=MESH)
    pl.semaphore_wait(barrier, len(devices))


def send(src, dst, send_sem, recv_sem, device):
    return pltpu.make_async_remote_copy(
        src_ref=src,
        dst_ref=dst,
        send_sem=send_sem,
        recv_sem=recv_sem,
        device_id=device,
        device_id_type=MESH,
    )


def spread_kernel(
    n,
    act_a,
    act_b,
    mat_a,
    mat_b,
    all_a,
    all_b,
    cut_a,
    cut_b,
    own_act,
    own_mat,
    local_sem,
    act_send,
    act_recv,
    mat_send,
    mat_recv,
):
    me = lax.axis_index("dp")
    col = lax.axis_index("mp")
    tokens = act_a.shape[0]
    part = tokens // 4
    rows = mat_a.shape[0]
    width = mat_a.shape[1] // n
    beside = flipped(me)
    core = flipped(col)
    across = lax.rem(col + 2, 4)
    acts = ((act_a, all_a), (act_b, all_b))
    mats = ((mat_a, cut_a), (mat_b, cut_b))
    others = [lax.rem(me + shift, n) for shift in range(1, n)]
    greet([(other, col) for other in others] + [(me, core), (me, across)])

    def rows_of(owner, quarter):
        return pl.ds(pl.multiple_of(owner * tokens + quarter * part, part), part)

    loads, stores = [], []
    for k in range(2):
        loads.append(pltpu.make_async_copy(acts[k][0], own_act.at[k], local_sem.at[k]))
        stores.append(
            pltpu.make_async_copy(
                own_act.at[k],
                acts[k][1].at[pl.ds(pl.multiple_of(me * tokens, tokens), tokens)],
                local_sem.at[k],
            )
        )
        cols = pl.ds(pl.multiple_of(me * width, width), width)
        loads.append(pltpu.make_async_copy(mats[k][0].at[:, cols], own_mat.at[k], local_sem.at[2 + k]))
        stores.append(
            pltpu.make_async_copy(
                own_mat.at[k],
                mats[k][1].at[pl.ds(pl.multiple_of(me * rows, rows), rows)],
                local_sem.at[2 + k],
            )
        )

    sent = []
    slots = [0]

    def post(k, src, owner, quarter, device):
        slot = slots[0]
        slots[0] += 1
        copy = send(
            src, acts[k][1].at[rows_of(owner, quarter)], act_send.at[slot], act_recv.at[slot], device
        )
        copy.start()
        sent.append(copy)
        return copy

    def own_rows(k):
        return acts[k][0].at[pl.ds(pl.multiple_of(col * part, part), part)]

    far = [lax.rem(me + 2 * shift, n) for shift in range(1, n // 2)]
    from_far = [lax.rem(me + n - 2 * shift, n) for shift in range(1, n // 2)]
    along = [[post(k, own_rows(k), me, col, (other, col)) for other in far] for k in range(2)]
    over = [[post(k, own_rows(k), me, col, (beside, col))] for k in range(2)]
    mat_sent = []
    for k in range(2):
        for shift in range(1, n):
            other = others[shift - 1]
            copy = send(
                mats[k][0].at[:, pl.ds(pl.multiple_of(other * width, width), width)],
                mats[k][1].at[pl.ds(pl.multiple_of(me * rows, rows), rows)],
                mat_send.at[k, shift - 1],
                mat_recv.at[k, shift - 1],
                (other, col),
            )
            copy.start()
            mat_sent.append(copy)
    for load in loads:
        load.start()
    for load, store in zip(loads, stores):
        load.wait()
        store.start()

    def held(k, owner, quarter):
        return acts[k][1].at[rows_of(owner, quarter)]

    crossed = [[], []]
    shared = [[], []]
    for k in range(2):
        for slot, owner in enumerate(from_far):
            along[k][slot].wait_recv()
            over[k].append(post(k, held(k, owner, col), owner, col, (beside, col)))
            crossed[k].append((owner, post(k, held(k, owner, col), owner, col, (me, across))))
            shared[k].append(post(k, held(k, owner, col), owner, col, (me, core)))
    for k in range(2):
        for copy, owner in zip(over[k], [beside] + [flipped(owner) for owner in from_far]):
            copy.wait_recv()
            crossed[k].append((owner, post(k, held(k, owner, col), owner, col, (me, across))))
            shared[k].append(post(k, held(k, owner, col), owner, col, (me, core)))
    for k in range(2):
        for owner, copy in crossed[k]:
            copy.wait_recv()
            shared[k].append(post(k, held(k, owner, across), owner, across, (me, core)))
    for k in range(2):
        for copy in shared[k]:
            copy.wait_recv()
    for copy in mat_sent:
        copy.wait_recv()
    for copy in sent + mat_sent:
        copy.wait_send()
    for store in stores:
        store.wait()


def spread(act_a, act_b, mat_a, mat_b):
    n = lax.axis_size("dp")
    tokens, depth = act_a.shape
    rows, width = mat_a.shape[0], mat_a.shape[1] // n
    slots = 2 * ((n // 2 - 1) + 1 + (n // 2 - 1) + (n - 1) + 2 * (n - 1))
    anywhere = pl.BlockSpec(memory_space=pl.ANY)
    return pl.pallas_call(
        functools.partial(spread_kernel, n),
        out_shape=(
            jax.ShapeDtypeStruct((tokens * n, depth), act_a.dtype),
            jax.ShapeDtypeStruct((tokens * n, depth), act_a.dtype),
            jax.ShapeDtypeStruct((rows * n, width), mat_a.dtype),
            jax.ShapeDtypeStruct((rows * n, width), mat_a.dtype),
        ),
        in_specs=[anywhere] * 4,
        out_specs=(anywhere,) * 4,
        scratch_shapes=[
            pltpu.VMEM((2, tokens, depth), act_a.dtype),
            pltpu.VMEM((2, rows, width), mat_a.dtype),
            pltpu.SemaphoreType.DMA((4,)),
            pltpu.SemaphoreType.DMA((slots,)),
            pltpu.SemaphoreType.DMA((slots,)),
            pltpu.SemaphoreType.DMA((2, n - 1)),
            pltpu.SemaphoreType.DMA((2, n - 1)),
        ],
        compiler_params=pltpu.CompilerParams(collective_id=0, has_side_effects=True),
    )(act_a, act_b, mat_a, mat_b)


def return_kernel(n, mat_a, mat_b, out_a, out_b, own_mat, local_sem, mat_send, mat_recv):
    me = lax.axis_index("dp")
    col = lax.axis_index("mp")
    rows, width = mat_a.shape[0] // n, mat_a.shape[1]
    others = [lax.rem(me + shift, n) for shift in range(1, n)]
    greet([(other, col) for other in others])
    mats = ((mat_a, out_a), (mat_b, out_b))
    cols = pl.ds(pl.multiple_of(me * width, width), width)
    sent = []
    for k in range(2):
        for shift in range(1, n):
            other = others[shift - 1]
            copy = send(
                mats[k][0].at[pl.ds(pl.multiple_of(other * rows, rows), rows)],
                mats[k][1].at[:, cols],
                mat_send.at[k, shift - 1],
                mat_recv.at[k, shift - 1],
                (other, col),
            )
            copy.start()
            sent.append(copy)
    loads, stores = [], []
    for k in range(2):
        mine = mats[k][0].at[pl.ds(pl.multiple_of(me * rows, rows), rows)]
        loads.append(pltpu.make_async_copy(mine, own_mat.at[k], local_sem.at[k]))
        stores.append(pltpu.make_async_copy(own_mat.at[k], mats[k][1].at[:, cols], local_sem.at[k]))
        loads[k].start()
    for load, store in zip(loads, stores):
        load.wait()
        store.start()
    for copy in sent:
        copy.wait()
    for store in stores:
        store.wait()


def returned(mat_a, mat_b):
    n = lax.axis_size("dp")
    rows, width = mat_a.shape[0] // n, mat_a.shape[1]
    anywhere = pl.BlockSpec(memory_space=pl.ANY)
    return pl.pallas_call(
        functools.partial(return_kernel, n),
        out_shape=(jax.ShapeDtypeStruct((rows, width * n), mat_a.dtype),) * 2,
        in_specs=[anywhere] * 2,
        out_specs=(anywhere,) * 2,
        scratch_shapes=[
            pltpu.VMEM((2, rows, width), mat_a.dtype),
            pltpu.SemaphoreType.DMA((2,)),
            pltpu.SemaphoreType.DMA((2, n - 1)),
            pltpu.SemaphoreType.DMA((2, n - 1)),
        ],
        compiler_params=pltpu.CompilerParams(collective_id=1, has_side_effects=True),
    )(mat_a, mat_b)


def suits_exchange(master, normed):
    n = lax.axis_size("dp")
    return (
        lax.axis_size("mp") == 4
        and 4 <= n <= 8
        and n % 2 == 0
        and master.shape[1] % (n * 128) == 0
        and master.shape[0] % 16 == 0
        and normed.shape[0] % 64 == 0
    )


def exchanged_grads(normed, out_grad, w_up, w_down):
    normed_all, out_grad_all, cut_up, cut_down = spread(normed, out_grad, w_up, w_down)
    pre_act = jnp.dot(normed_all, cut_up, preferred_element_type=jnp.float32)
    act_value, pull_back = jax.vjp(gelu_tanh, pre_act)
    hidden_act = act_value.astype(jnp.bfloat16)
    act_grad = jnp.dot(out_grad_all, cut_down, preferred_element_type=jnp.float32)
    pre_grad = pull_back(act_grad)[0].astype(jnp.bfloat16)
    grad_up = contract_tokens(normed_all, pre_grad).astype(jnp.bfloat16)
    grad_down = contract_tokens(out_grad_all, hidden_act).astype(jnp.bfloat16)
    grad_up, grad_down = returned(grad_up, grad_down)
    return grad_up.astype(jnp.float32), grad_down.astype(jnp.float32)


def on_device(
    token_pool,
    visible,
    out_grad,
    ln_gain,
    master_up,
    master_down,
    row_up,
    col_up,
    row_down,
    col_down,
):
    picked = jnp.take(token_pool, visible, axis=0).astype(jnp.float32)
    normed = normalize(picked, ln_gain)
    grid_rows = master_up.shape[0]
    grid_cols = master_up.shape[1]
    depth = grid_rows * lax.axis_size("dp")
    breadth = grid_cols * lax.axis_size("mp")
    w_up = master_up.astype(jnp.bfloat16)
    w_down = master_down.astype(jnp.bfloat16)
    if suits_exchange(master_up, normed):
        grad_up, grad_down = exchanged_grads(normed, out_grad, w_up, w_down)
    else:
        grad_up, grad_down = gathered_grads(normed, out_grad, w_up, w_down)
    squares_up = grad_up * grad_up + tiny_value
    squares_down = grad_down * grad_down + tiny_value
    rowpart_up = jnp.sum(squares_up, axis=1)
    rowpart_down = jnp.sum(squares_down, axis=1)
    colpart_up = jnp.sum(squares_up, axis=0)
    colpart_down = jnp.sum(squares_down, axis=0)
    rowsum_up, rowsum_down = lax.psum((rowpart_up, rowpart_down), "mp")
    colsum_up, colsum_down = lax.psum((colpart_up, colpart_down), "dp")
    row_up_new = decay_rate * row_up + (1.0 - decay_rate) * rowsum_up / breadth
    row_down_new = decay_rate * row_down + (1.0 - decay_rate) * rowsum_down / breadth
    col_up_new = decay_rate * col_up + (1.0 - decay_rate) * colsum_up / depth
    col_down_new = decay_rate * col_down + (1.0 - decay_rate) * colsum_down / depth
    raw_up = finish_update(grad_up, row_up_new, col_up_new)
    raw_down = finish_update(grad_down, row_down_new, col_down_new)
    energy_up, energy_down = lax.psum(
        (jnp.sum(raw_up * raw_up), jnp.sum(raw_down * raw_down)), ("dp", "mp")
    )
    update_up = raw_up / jnp.maximum(1.0, jnp.sqrt(energy_up / (depth * breadth)))
    update_down = raw_down / jnp.maximum(1.0, jnp.sqrt(energy_down / (depth * breadth)))
    return (update_up, update_down, row_up_new, col_up_new, row_down_new, col_down_new)


def solution(mesh):
    return jax.shard_map(
        on_device,
        mesh=mesh,
        in_specs=(
            P("dp", None),
            P("dp"),
            P("dp", None),
            P(),
            P("dp", "mp"),
            P("dp", "mp"),
            P("dp"),
            P("mp"),
            P("dp"),
            P("mp"),
        ),
        out_specs=(P("dp", "mp"), P("dp", "mp"), P("dp"), P("mp"), P("dp"), P("mp")),
        check_vma=False,
    )
```

```python
import functools
import jax
import jax.numpy as jnp
from jax import lax
from jax.experimental import pallas as pl
from jax.experimental.pallas import tpu as pltpu
from jax.sharding import PartitionSpec as P

decay_rate = 0.8
norm_eps = 1e-06
tiny_value = 1e-30


def gelu_tanh(values):
    return jax.nn.gelu(values, approximate=True)


def normalize(values, gain):
    mean_val = jnp.mean(values, axis=1, keepdims=True)
    centred = values - mean_val
    variance = jnp.mean(centred * centred, axis=1, keepdims=True)
    return (centred * lax.rsqrt(variance + norm_eps) * gain).astype(jnp.bfloat16)


def contract_tokens(left, right):
    return lax.dot_general(
        left, right, (((0,), (0,)), ((), ())), preferred_element_type=jnp.float32
    )


def finish_update(grad, row_new, col_new):
    return grad * lax.rsqrt(row_new[:, None] * col_new[None, :])


def gathered_grads(normed, out_grad, w_up, w_down):
    left = normed
    pre_act = jnp.dot(
        left, lax.all_gather(w_up, "dp", axis=0, tiled=True), preferred_element_type=jnp.float32
    )
    act_value, pull_back = jax.vjp(gelu_tanh, pre_act)
    hidden_act = act_value.astype(jnp.bfloat16)
    left = out_grad
    act_grad = jnp.dot(
        left, lax.all_gather(w_down, "dp", axis=0, tiled=True), preferred_element_type=jnp.float32
    )
    pre_grad = pull_back(act_grad)[0].astype(jnp.bfloat16)
    grad_down = lax.psum_scatter(
        contract_tokens(out_grad, hidden_act), "dp", scatter_dimension=0, tiled=True
    )
    grad_up = lax.psum_scatter(
        contract_tokens(normed, pre_grad), "dp", scatter_dimension=0, tiled=True
    )
    return grad_up, grad_down


MESH = pl.DeviceIdType.MESH


def flipped(index):
    return index + 1 - 2 * lax.rem(index, 2)


def greet(devices):
    barrier = pltpu.get_barrier_semaphore()
    for device in devices:
        pl.semaphore_signal(barrier, inc=1, device_id=device, device_id_type=MESH)
    pl.semaphore_wait(barrier, len(devices))


def send(src, dst, send_sem, recv_sem, device):
    return pltpu.make_async_remote_copy(
        src_ref=src,
        dst_ref=dst,
        send_sem=send_sem,
        recv_sem=recv_sem,
        device_id=device,
        device_id_type=MESH,
    )


def spread_kernel(
    n,
    act_a,
    act_b,
    mat_a,
    mat_b,
    all_a,
    all_b,
    cut_a,
    cut_b,
    own_act,
    own_mat,
    local_sem,
    act_send,
    act_recv,
    mat_send,
    mat_recv,
):
    me = lax.axis_index("dp")
    col = lax.axis_index("mp")
    tokens = act_a.shape[0]
    part = tokens // 4
    rows = mat_a.shape[0]
    width = mat_a.shape[1] // n
    beside = flipped(me)
    core = flipped(col)
    across = lax.rem(col + 2, 4)
    acts = ((act_a, all_a), (act_b, all_b))
    mats = ((mat_a, cut_a), (mat_b, cut_b))
    others = [lax.rem(me + shift, n) for shift in range(1, n)]
    greet([(other, col) for other in others] + [(me, core), (me, across)])

    def rows_of(owner, quarter):
        return pl.ds(pl.multiple_of(owner * tokens + quarter * part, part), part)

    loads, stores = [], []
    for k in range(2):
        loads.append(pltpu.make_async_copy(acts[k][0], own_act.at[k], local_sem.at[k]))
        stores.append(
            pltpu.make_async_copy(
                own_act.at[k],
                acts[k][1].at[pl.ds(pl.multiple_of(me * tokens, tokens), tokens)],
                local_sem.at[k],
            )
        )
        cols = pl.ds(pl.multiple_of(me * width, width), width)
        loads.append(pltpu.make_async_copy(mats[k][0].at[:, cols], own_mat.at[k], local_sem.at[2 + k]))
        stores.append(
            pltpu.make_async_copy(
                own_mat.at[k],
                mats[k][1].at[pl.ds(pl.multiple_of(me * rows, rows), rows)],
                local_sem.at[2 + k],
            )
        )

    sent = []
    slots = [0]

    def post(k, src, owner, quarter, device):
        slot = slots[0]
        slots[0] += 1
        copy = send(
            src, acts[k][1].at[rows_of(owner, quarter)], act_send.at[slot], act_recv.at[slot], device
        )
        copy.start()
        sent.append(copy)
        return copy

    def own_rows(k):
        return acts[k][0].at[pl.ds(pl.multiple_of(col * part, part), part)]

    far = [lax.rem(me + 2 * shift, n) for shift in range(1, n // 2)]
    from_far = [lax.rem(me + n - 2 * shift, n) for shift in range(1, n // 2)]
    along = [[post(k, own_rows(k), me, col, (other, col)) for other in far] for k in range(2)]
    over = [[post(k, own_rows(k), me, col, (beside, col))] for k in range(2)]
    mat_sent = []
    for k in range(2):
        for shift in range(1, n):
            other = others[shift - 1]
            copy = send(
                mats[k][0].at[:, pl.ds(pl.multiple_of(other * width, width), width)],
                mats[k][1].at[pl.ds(pl.multiple_of(me * rows, rows), rows)],
                mat_send.at[k, shift - 1],
                mat_recv.at[k, shift - 1],
                (other, col),
            )
            copy.start()
            mat_sent.append(copy)
    for load in loads:
        load.start()
    for load, store in zip(loads, stores):
        load.wait()
        store.start()

    def held(k, owner, quarter):
        return acts[k][1].at[rows_of(owner, quarter)]

    crossed = [[], []]
    shared = [[], []]
    for k in range(2):
        for slot, owner in enumerate(from_far):
            along[k][slot].wait_recv()
            over[k].append(post(k, held(k, owner, col), owner, col, (beside, col)))
            crossed[k].append((owner, post(k, held(k, owner, col), owner, col, (me, across))))
            shared[k].append(post(k, held(k, owner, col), owner, col, (me, core)))
    for k in range(2):
        for copy, owner in zip(over[k], [beside] + [flipped(owner) for owner in from_far]):
            copy.wait_recv()
            crossed[k].append((owner, post(k, held(k, owner, col), owner, col, (me, across))))
            shared[k].append(post(k, held(k, owner, col), owner, col, (me, core)))
    for k in range(2):
        for owner, copy in crossed[k]:
            copy.wait_recv()
            shared[k].append(post(k, held(k, owner, across), owner, across, (me, core)))
    for k in range(2):
        for copy in shared[k]:
            copy.wait_recv()
    for copy in mat_sent:
        copy.wait_recv()
    for copy in sent + mat_sent:
        copy.wait_send()
    for store in stores:
        store.wait()


def spread(act_a, act_b, mat_a, mat_b):
    n = lax.axis_size("dp")
    tokens, depth = act_a.shape
    rows, width = mat_a.shape[0], mat_a.shape[1] // n
    slots = 2 * ((n // 2 - 1) + 1 + (n // 2 - 1) + (n - 1) + 2 * (n - 1))
    anywhere = pl.BlockSpec(memory_space=pl.ANY)
    return pl.pallas_call(
        functools.partial(spread_kernel, n),
        out_shape=(
            jax.ShapeDtypeStruct((tokens * n, depth), act_a.dtype),
            jax.ShapeDtypeStruct((tokens * n, depth), act_a.dtype),
            jax.ShapeDtypeStruct((rows * n, width), mat_a.dtype),
            jax.ShapeDtypeStruct((rows * n, width), mat_a.dtype),
        ),
        in_specs=[anywhere] * 4,
        out_specs=(anywhere,) * 4,
        scratch_shapes=[
            pltpu.VMEM((2, tokens, depth), act_a.dtype),
            pltpu.VMEM((2, rows, width), mat_a.dtype),
            pltpu.SemaphoreType.DMA((4,)),
            pltpu.SemaphoreType.DMA((slots,)),
            pltpu.SemaphoreType.DMA((slots,)),
            pltpu.SemaphoreType.DMA((2, n - 1)),
            pltpu.SemaphoreType.DMA((2, n - 1)),
        ],
        compiler_params=pltpu.CompilerParams(collective_id=0, has_side_effects=True),
    )(act_a, act_b, mat_a, mat_b)


def return_kernel(
    n,
    breadth,
    mat_a,
    mat_b,
    stats,
    row_old,
    out_a,
    out_b,
    gathered,
    row_new,
    energy,
    own_mat,
    stat_buf,
    line_buf,
    energy_buf,
    local_sem,
    mat_send,
    mat_recv,
    stat_send,
    stat_recv,
    line_send,
    line_recv,
    energy_send,
    energy_recv,
):
    me = lax.axis_index("dp")
    col = lax.axis_index("mp")
    rows, width = mat_a.shape[0] // n, mat_a.shape[1]
    others = [lax.rem(me + shift, n) for shift in range(1, n)]
    sources = [lax.rem(me + n - shift, n) for shift in range(1, n)]
    siblings = [lax.rem(col + shift, 4) for shift in range(1, 4)]
    greet([(other, col) for other in others] + [(me, other) for other in siblings])
    mats = ((mat_a, out_a), (mat_b, out_b))
    cols = pl.ds(pl.multiple_of(me * width, width), width)
    stat_sent = []
    for shift, other in enumerate(others):
        copy = send(
            stats.at[other], stat_buf.at[me], stat_send.at[shift], stat_recv.at[shift], (other, col)
        )
        copy.start()
        stat_sent.append(copy)
    sent = [[], []]
    for k in range(2):
        for shift in range(1, n):
            other = others[shift - 1]
            copy = send(
                mats[k][0].at[pl.ds(pl.multiple_of(other * rows, rows), rows)],
                mats[k][1].at[:, cols],
                mat_send.at[k, shift - 1],
                mat_recv.at[k, shift - 1],
                (other, col),
            )
            copy.start()
            sent[k].append(copy)
    loads, stores = [], []
    for k in range(2):
        mine = mats[k][0].at[pl.ds(pl.multiple_of(me * rows, rows), rows)]
        loads.append(pltpu.make_async_copy(mine, own_mat.at[k], local_sem.at[k]))
        stores.append(pltpu.make_async_copy(own_mat.at[k], mats[k][1].at[:, cols], local_sem.at[k]))
        loads[k].start()

    for copy in stat_sent:
        copy.wait_recv()
    total = stats[me]
    gathered[me] = total
    for source in sources:
        block = stat_buf[source]
        gathered[source] = block
        total = total + block
    line_buf[col] = total
    for load, store in zip(loads, stores):
        load.wait()
        store.start()
    for store in stores:
        store.wait()
    line_sent = []
    for shift, other in enumerate(siblings):
        copy = send(
            line_buf.at[col], line_buf.at[col], line_send.at[shift], line_recv.at[shift], (me, other)
        )
        copy.start()
        line_sent.append(copy)
    for copy in line_sent:
        copy.wait_recv()
    total = line_buf[0] + line_buf[1] + line_buf[2] + line_buf[3]
    fresh = decay_rate * row_old[...] + (1.0 - decay_rate) * total[0:2] / breadth
    row_new[0:2] = fresh
    spent = jnp.sum(total[2:4] / fresh, axis=1, keepdims=True)
    energy_buf[me] = jnp.broadcast_to(spent, (2, 128))
    for copy in stat_sent + line_sent:
        copy.wait_send()
    sent[0][0].wait_recv()
    energy_sent = []
    for shift, other in enumerate(others):
        copy = send(
            energy_buf.at[me], energy_buf.at[me], energy_send.at[shift], energy_recv.at[shift], (other, col)
        )
        copy.start()
        energy_sent.append(copy)
    for copy in sent[0][1:] + sent[1] + energy_sent:
        copy.wait_recv()
    summed = energy_buf[0]
    for source in range(1, n):
        summed = summed + energy_buf[source]
    energy[...] = summed
    for copy in sent[0] + sent[1] + energy_sent:
        copy.wait_send()


def returned(mat_a, mat_b, stats, row_old, breadth):
    n = lax.axis_size("dp")
    rows, width = mat_a.shape[0] // n, mat_a.shape[1]
    anywhere = pl.BlockSpec(memory_space=pl.ANY)
    vmem = pl.BlockSpec(memory_space=pltpu.VMEM)
    peers = pltpu.SemaphoreType.DMA((n - 1,))
    line = pltpu.SemaphoreType.DMA((3,))
    return pl.pallas_call(
        functools.partial(return_kernel, n, breadth),
        out_shape=(
            jax.ShapeDtypeStruct((rows, width * n), mat_a.dtype),
            jax.ShapeDtypeStruct((rows, width * n), mat_a.dtype),
            jax.ShapeDtypeStruct(stats.shape, jnp.float32),
            jax.ShapeDtypeStruct(row_old.shape, jnp.float32),
            jax.ShapeDtypeStruct((2, 128), jnp.float32),
        ),
        in_specs=[anywhere, anywhere, vmem, vmem],
        out_specs=(anywhere, anywhere, vmem, vmem, vmem),
        scratch_shapes=[
            pltpu.VMEM((2, rows, width), mat_a.dtype),
            pltpu.VMEM(stats.shape, jnp.float32),
            pltpu.VMEM((4,) + stats.shape[1:], jnp.float32),
            pltpu.VMEM((n, 2, 128), jnp.float32),
            pltpu.SemaphoreType.DMA((2,)),
            pltpu.SemaphoreType.DMA((2, n - 1)),
            pltpu.SemaphoreType.DMA((2, n - 1)),
            peers,
            peers,
            line,
            line,
            peers,
            peers,
        ],
        compiler_params=pltpu.CompilerParams(collective_id=1, has_side_effects=True),
    )(mat_a, mat_b, stats, row_old)


def suits_exchange(master, normed):
    n = lax.axis_size("dp")
    return (
        lax.axis_size("mp") == 4
        and 4 <= n <= 8
        and n % 2 == 0
        and master.shape[1] % (n * 128) == 0
        and master.shape[0] % 16 == 0
        and master.shape[0] * n == master.shape[1]
        and normed.shape[0] % 64 == 0
    )


def column_block(grad, col_old, depth):
    width = grad.shape[1]
    mine = lax.dynamic_slice_in_dim(col_old, lax.axis_index("dp") * width, width)
    squares = grad * grad + tiny_value
    col_new = decay_rate * mine + (1.0 - decay_rate) * jnp.sum(squares, axis=0) / depth
    rowpart = jnp.sum(squares, axis=1)
    spent = jnp.sum(grad * grad * (1.0 / col_new)[None, :], axis=1)
    return rowpart, spent, col_new


def exchanged_step(normed, out_grad, w_up, w_down, row_up, col_up, row_down, col_down):
    n = lax.axis_size("dp")
    rows, width = w_up.shape[0], w_up.shape[1] // n
    depth = rows * n
    breadth = width * n * lax.axis_size("mp")
    normed_all, out_grad_all, cut_up, cut_down = spread(normed, out_grad, w_up, w_down)
    pre_act = jnp.dot(normed_all, cut_up, preferred_element_type=jnp.float32)
    act_value, pull_back = jax.vjp(gelu_tanh, pre_act)
    hidden_act = act_value.astype(jnp.bfloat16)
    act_grad = jnp.dot(out_grad_all, cut_down, preferred_element_type=jnp.float32)
    pre_grad = pull_back(act_grad)[0].astype(jnp.bfloat16)
    grad_down = contract_tokens(out_grad_all, hidden_act)
    grad_up = contract_tokens(normed_all, pre_grad)
    rowpart_up, spent_up, col_part_up = column_block(grad_up, col_up, depth)
    rowpart_down, spent_down, col_part_down = column_block(grad_down, col_down, depth)
    by_row = jnp.stack([rowpart_up, rowpart_down, spent_up, spent_down]).reshape(4, n, rows)
    by_col = jnp.broadcast_to(jnp.stack([col_part_up, col_part_down])[:, None], (2, n, width))
    stats = jnp.concatenate([by_row, by_col, jnp.zeros_like(by_col)]).transpose(1, 0, 2)
    moved_up, moved_down, gathered, row_new, energy = returned(
        grad_up.astype(jnp.bfloat16),
        grad_down.astype(jnp.bfloat16),
        stats,
        jnp.stack([row_up, row_down]),
        breadth,
    )
    col_new = gathered[:, 4:6].transpose(1, 0, 2).reshape(2, n * width)
    shrink = jnp.maximum(1.0, jnp.sqrt(energy[:, 0] / (depth * breadth)))
    update_up = finish_update(moved_up.astype(jnp.float32), row_new[0], col_new[0]) / shrink[0]
    update_down = finish_update(moved_down.astype(jnp.float32), row_new[1], col_new[1]) / shrink[1]
    return (update_up, update_down, row_new[0], col_new[0], row_new[1], col_new[1])


def on_device(
    token_pool,
    visible,
    out_grad,
    ln_gain,
    master_up,
    master_down,
    row_up,
    col_up,
    row_down,
    col_down,
):
    picked = jnp.take(token_pool, visible, axis=0).astype(jnp.float32)
    normed = normalize(picked, ln_gain)
    grid_rows = master_up.shape[0]
    grid_cols = master_up.shape[1]
    depth = grid_rows * lax.axis_size("dp")
    breadth = grid_cols * lax.axis_size("mp")
    w_up = master_up.astype(jnp.bfloat16)
    w_down = master_down.astype(jnp.bfloat16)
    if suits_exchange(master_up, normed):
        return exchanged_step(normed, out_grad, w_up, w_down, row_up, col_up, row_down, col_down)
    grad_up, grad_down = gathered_grads(normed, out_grad, w_up, w_down)
    squares_up = grad_up * grad_up + tiny_value
    squares_down = grad_down * grad_down + tiny_value
    rowpart_up = jnp.sum(squares_up, axis=1)
    rowpart_down = jnp.sum(squares_down, axis=1)
    colpart_up = jnp.sum(squares_up, axis=0)
    colpart_down = jnp.sum(squares_down, axis=0)
    rowsum_up, rowsum_down = lax.psum((rowpart_up, rowpart_down), "mp")
    colsum_up, colsum_down = lax.psum((colpart_up, colpart_down), "dp")
    row_up_new = decay_rate * row_up + (1.0 - decay_rate) * rowsum_up / breadth
    row_down_new = decay_rate * row_down + (1.0 - decay_rate) * rowsum_down / breadth
    col_up_new = decay_rate * col_up + (1.0 - decay_rate) * colsum_up / depth
    col_down_new = decay_rate * col_down + (1.0 - decay_rate) * colsum_down / depth
    raw_up = finish_update(grad_up, row_up_new, col_up_new)
    raw_down = finish_update(grad_down, row_down_new, col_down_new)
    energy_up, energy_down = lax.psum(
        (jnp.sum(raw_up * raw_up), jnp.sum(raw_down * raw_down)), ("dp", "mp")
    )
    update_up = raw_up / jnp.maximum(1.0, jnp.sqrt(energy_up / (depth * breadth)))
    update_down = raw_down / jnp.maximum(1.0, jnp.sqrt(energy_down / (depth * breadth)))
    return (update_up, update_down, row_up_new, col_up_new, row_down_new, col_down_new)


def solution(mesh):
    return jax.shard_map(
        on_device,
        mesh=mesh,
        in_specs=(
            P("dp", None),
            P("dp"),
            P("dp", None),
            P(),
            P("dp", "mp"),
            P("dp", "mp"),
            P("dp"),
            P("mp"),
            P("dp"),
            P("mp"),
        ),
        out_specs=(P("dp", "mp"), P("dp", "mp"), P("dp"), P("mp"), P("dp"), P("mp")),
        check_vma=False,
    )
```

```python
import functools
import jax
import jax.numpy as jnp
from jax import lax
from jax.experimental import pallas as pl
from jax.experimental.pallas import tpu as pltpu
from jax.sharding import PartitionSpec as P

decay_rate = 0.8
norm_eps = 1e-06
tiny_value = 1e-30


def gelu_tanh(values):
    return jax.nn.gelu(values, approximate=True)


def normalize(values, gain):
    mean_val = jnp.mean(values, axis=1, keepdims=True)
    centred = values - mean_val
    variance = jnp.mean(centred * centred, axis=1, keepdims=True)
    return (centred * lax.rsqrt(variance + norm_eps) * gain).astype(jnp.bfloat16)


def contract_tokens(left, right):
    return lax.dot_general(
        left, right, (((0,), (0,)), ((), ())), preferred_element_type=jnp.float32
    )


def finish_update(grad, row_new, col_new):
    return grad * lax.rsqrt(row_new[:, None] * col_new[None, :])


def gathered_grads(normed, out_grad, w_up, w_down):
    left = normed
    pre_act = jnp.dot(
        left, lax.all_gather(w_up, "dp", axis=0, tiled=True), preferred_element_type=jnp.float32
    )
    act_value, pull_back = jax.vjp(gelu_tanh, pre_act)
    hidden_act = act_value.astype(jnp.bfloat16)
    left = out_grad
    act_grad = jnp.dot(
        left, lax.all_gather(w_down, "dp", axis=0, tiled=True), preferred_element_type=jnp.float32
    )
    pre_grad = pull_back(act_grad)[0].astype(jnp.bfloat16)
    grad_down = lax.psum_scatter(
        contract_tokens(out_grad, hidden_act), "dp", scatter_dimension=0, tiled=True
    )
    grad_up = lax.psum_scatter(
        contract_tokens(normed, pre_grad), "dp", scatter_dimension=0, tiled=True
    )
    return grad_up, grad_down


MESH = pl.DeviceIdType.MESH


def flipped(index):
    return index + 1 - 2 * lax.rem(index, 2)


def greet(devices):
    barrier = pltpu.get_barrier_semaphore()
    for device in devices:
        pl.semaphore_signal(barrier, inc=1, device_id=device, device_id_type=MESH)
    pl.semaphore_wait(barrier, len(devices))


def send(src, dst, send_sem, recv_sem, device):
    return pltpu.make_async_remote_copy(
        src_ref=src,
        dst_ref=dst,
        send_sem=send_sem,
        recv_sem=recv_sem,
        device_id=device,
        device_id_type=MESH,
    )


def spread_kernel(
    n,
    act_a,
    act_b,
    mat_a,
    mat_b,
    all_a,
    all_b,
    cut_a,
    cut_b,
    own_act,
    own_mat,
    local_sem,
    act_send,
    act_recv,
    mat_send,
    mat_recv,
):
    me = lax.axis_index("dp")
    col = lax.axis_index("mp")
    tokens = act_a.shape[0]
    part = tokens // 4
    rows = mat_a.shape[0]
    width = mat_a.shape[1] // n
    beside = flipped(me)
    core = flipped(col)
    across = lax.rem(col + 2, 4)
    acts = ((act_a, all_a), (act_b, all_b))
    mats = ((mat_a, cut_a), (mat_b, cut_b))
    others = [lax.rem(me + shift, n) for shift in range(1, n)]
    greet([(other, col) for other in others] + [(me, core), (me, across)])

    def rows_of(owner, quarter):
        return pl.ds(pl.multiple_of(owner * tokens + quarter * part, part), part)

    loads, stores = [], []
    for k in range(2):
        loads.append(pltpu.make_async_copy(acts[k][0], own_act.at[k], local_sem.at[k]))
        stores.append(
            pltpu.make_async_copy(
                own_act.at[k],
                acts[k][1].at[pl.ds(pl.multiple_of(me * tokens, tokens), tokens)],
                local_sem.at[k],
            )
        )
        cols = pl.ds(pl.multiple_of(me * width, width), width)
        loads.append(pltpu.make_async_copy(mats[k][0].at[:, cols], own_mat.at[k], local_sem.at[2 + k]))
        stores.append(
            pltpu.make_async_copy(
                own_mat.at[k],
                mats[k][1].at[pl.ds(pl.multiple_of(me * rows, rows), rows)],
                local_sem.at[2 + k],
            )
        )

    sent = []
    slots = [0]

    def post(k, src, owner, quarter, device):
        slot = slots[0]
        slots[0] += 1
        copy = send(
            src, acts[k][1].at[rows_of(owner, quarter)], act_send.at[slot], act_recv.at[slot], device
        )
        copy.start()
        sent.append(copy)
        return copy

    def own_rows(k):
        return acts[k][0].at[pl.ds(pl.multiple_of(col * part, part), part)]

    far = [lax.rem(me + 2 * shift, n) for shift in range(1, n // 2)]
    from_far = [lax.rem(me + n - 2 * shift, n) for shift in range(1, n // 2)]
    along = [[post(k, own_rows(k), me, col, (other, col)) for other in far] for k in range(2)]
    over = [[post(k, own_rows(k), me, col, (beside, col))] for k in range(2)]
    mat_sent = []

    def post_mats(k):
        for shift in range(1, n):
            other = others[shift - 1]
            copy = send(
                mats[k][0].at[:, pl.ds(pl.multiple_of(other * width, width), width)],
                mats[k][1].at[pl.ds(pl.multiple_of(me * rows, rows), rows)],
                mat_send.at[k, shift - 1],
                mat_recv.at[k, shift - 1],
                (other, col),
            )
            copy.start()
            mat_sent.append(copy)

    post_mats(0)
    for load in loads:
        load.start()
    for load, store in zip(loads, stores):
        load.wait()
        store.start()

    def held(k, owner, quarter):
        return acts[k][1].at[rows_of(owner, quarter)]

    crossed = [[], []]
    shared = [[], []]
    for k in range(2):
        for slot, owner in enumerate(from_far):
            along[k][slot].wait_recv()
            over[k].append(post(k, held(k, owner, col), owner, col, (beside, col)))
            crossed[k].append((owner, post(k, held(k, owner, col), owner, col, (me, across))))
            shared[k].append(post(k, held(k, owner, col), owner, col, (me, core)))
    post_mats(1)
    for k in range(2):
        for copy, owner in zip(over[k], [beside] + [flipped(owner) for owner in from_far]):
            copy.wait_recv()
            crossed[k].append((owner, post(k, held(k, owner, col), owner, col, (me, across))))
            shared[k].append(post(k, held(k, owner, col), owner, col, (me, core)))
    for k in range(2):
        for owner, copy in crossed[k]:
            copy.wait_recv()
            shared[k].append(post(k, held(k, owner, across), owner, across, (me, core)))
    for k in range(2):
        for copy in shared[k]:
            copy.wait_recv()
    for copy in mat_sent:
        copy.wait_recv()
    for copy in sent + mat_sent:
        copy.wait_send()
    for store in stores:
        store.wait()


def spread(act_a, act_b, mat_a, mat_b):
    n = lax.axis_size("dp")
    tokens, depth = act_a.shape
    rows, width = mat_a.shape[0], mat_a.shape[1] // n
    slots = 2 * ((n // 2 - 1) + 1 + (n // 2 - 1) + (n - 1) + 2 * (n - 1))
    anywhere = pl.BlockSpec(memory_space=pl.ANY)
    return pl.pallas_call(
        functools.partial(spread_kernel, n),
        out_shape=(
            jax.ShapeDtypeStruct((tokens * n, depth), act_a.dtype),
            jax.ShapeDtypeStruct((tokens * n, depth), act_a.dtype),
            jax.ShapeDtypeStruct((rows * n, width), mat_a.dtype),
            jax.ShapeDtypeStruct((rows * n, width), mat_a.dtype),
        ),
        in_specs=[anywhere] * 4,
        out_specs=(anywhere,) * 4,
        scratch_shapes=[
            pltpu.VMEM((2, tokens, depth), act_a.dtype),
            pltpu.VMEM((2, rows, width), mat_a.dtype),
            pltpu.SemaphoreType.DMA((4,)),
            pltpu.SemaphoreType.DMA((slots,)),
            pltpu.SemaphoreType.DMA((slots,)),
            pltpu.SemaphoreType.DMA((2, n - 1)),
            pltpu.SemaphoreType.DMA((2, n - 1)),
        ],
        compiler_params=pltpu.CompilerParams(collective_id=0, has_side_effects=True),
    )(act_a, act_b, mat_a, mat_b)


def return_kernel(
    n,
    breadth,
    mat_a,
    mat_b,
    stats,
    row_old,
    out_a,
    out_b,
    gathered,
    row_new,
    energy,
    own_mat,
    stat_buf,
    line_buf,
    energy_buf,
    local_sem,
    mat_send,
    mat_recv,
    stat_send,
    stat_recv,
    line_send,
    line_recv,
    energy_send,
    energy_recv,
):
    me = lax.axis_index("dp")
    col = lax.axis_index("mp")
    rows, width = mat_a.shape[0] // n, mat_a.shape[1]
    others = [lax.rem(me + shift, n) for shift in range(1, n)]
    sources = [lax.rem(me + n - shift, n) for shift in range(1, n)]
    siblings = [lax.rem(col + shift, 4) for shift in range(1, 4)]
    greet([(other, col) for other in others] + [(me, other) for other in siblings])
    mats = ((mat_a, out_a), (mat_b, out_b))
    cols = pl.ds(pl.multiple_of(me * width, width), width)
    stat_sent = []
    for shift, other in enumerate(others):
        copy = send(
            stats.at[other], stat_buf.at[me], stat_send.at[shift], stat_recv.at[shift], (other, col)
        )
        copy.start()
        stat_sent.append(copy)
    sent = [[], []]
    for k in range(2):
        for shift in range(1, n):
            other = others[shift - 1]
            copy = send(
                mats[k][0].at[pl.ds(pl.multiple_of(other * rows, rows), rows)],
                mats[k][1].at[:, cols],
                mat_send.at[k, shift - 1],
                mat_recv.at[k, shift - 1],
                (other, col),
            )
            copy.start()
            sent[k].append(copy)
    loads, stores = [], []
    for k in range(2):
        mine = mats[k][0].at[pl.ds(pl.multiple_of(me * rows, rows), rows)]
        loads.append(pltpu.make_async_copy(mine, own_mat.at[k], local_sem.at[k]))
        stores.append(pltpu.make_async_copy(own_mat.at[k], mats[k][1].at[:, cols], local_sem.at[k]))
        loads[k].start()

    for copy in stat_sent:
        copy.wait_recv()
    total = stats[me]
    gathered[me] = total
    for source in sources:
        block = stat_buf[source]
        gathered[source] = block
        total = total + block
    line_buf[col] = total
    for load, store in zip(loads, stores):
        load.wait()
        store.start()
    for store in stores:
        store.wait()
    line_sent = []
    for shift, other in enumerate(siblings):
        copy = send(
            line_buf.at[col], line_buf.at[col], line_send.at[shift], line_recv.at[shift], (me, other)
        )
        copy.start()
        line_sent.append(copy)
    for copy in line_sent:
        copy.wait_recv()
    total = line_buf[0] + line_buf[1] + line_buf[2] + line_buf[3]
    fresh = decay_rate * row_old[...] + (1.0 - decay_rate) * total[0:2] / breadth
    row_new[0:2] = fresh
    spent = jnp.sum(total[2:4] / fresh, axis=1, keepdims=True)
    energy_buf[me] = jnp.broadcast_to(spent, (2, 128))
    for copy in stat_sent + line_sent:
        copy.wait_send()
    sent[0][0].wait_recv()
    energy_sent = []
    for shift, other in enumerate(others):
        copy = send(
            energy_buf.at[me], energy_buf.at[me], energy_send.at[shift], energy_recv.at[shift], (other, col)
        )
        copy.start()
        energy_sent.append(copy)
    for copy in sent[0][1:] + sent[1] + energy_sent:
        copy.wait_recv()
    summed = energy_buf[0]
    for source in range(1, n):
        summed = summed + energy_buf[source]
    energy[...] = summed
    for copy in sent[0] + sent[1] + energy_sent:
        copy.wait_send()


def returned(mat_a, mat_b, stats, row_old, breadth):
    n = lax.axis_size("dp")
    rows, width = mat_a.shape[0] // n, mat_a.shape[1]
    anywhere = pl.BlockSpec(memory_space=pl.ANY)
    vmem = pl.BlockSpec(memory_space=pltpu.VMEM)
    peers = pltpu.SemaphoreType.DMA((n - 1,))
    line = pltpu.SemaphoreType.DMA((3,))
    return pl.pallas_call(
        functools.partial(return_kernel, n, breadth),
        out_shape=(
            jax.ShapeDtypeStruct((rows, width * n), mat_a.dtype),
            jax.ShapeDtypeStruct((rows, width * n), mat_a.dtype),
            jax.ShapeDtypeStruct(stats.shape, jnp.float32),
            jax.ShapeDtypeStruct(row_old.shape, jnp.float32),
            jax.ShapeDtypeStruct((2, 128), jnp.float32),
        ),
        in_specs=[anywhere, anywhere, vmem, vmem],
        out_specs=(anywhere, anywhere, vmem, vmem, vmem),
        scratch_shapes=[
            pltpu.VMEM((2, rows, width), mat_a.dtype),
            pltpu.VMEM(stats.shape, jnp.float32),
            pltpu.VMEM((4,) + stats.shape[1:], jnp.float32),
            pltpu.VMEM((n, 2, 128), jnp.float32),
            pltpu.SemaphoreType.DMA((2,)),
            pltpu.SemaphoreType.DMA((2, n - 1)),
            pltpu.SemaphoreType.DMA((2, n - 1)),
            peers,
            peers,
            line,
            line,
            peers,
            peers,
        ],
        compiler_params=pltpu.CompilerParams(collective_id=1, has_side_effects=True),
    )(mat_a, mat_b, stats, row_old)


def suits_exchange(master, normed):
    n = lax.axis_size("dp")
    return (
        lax.axis_size("mp") == 4
        and 4 <= n <= 8
        and n % 2 == 0
        and master.shape[1] % (n * 128) == 0
        and master.shape[0] % 16 == 0
        and master.shape[0] * n == master.shape[1]
        and normed.shape[0] % 64 == 0
    )


def column_block(grad, col_old, depth):
    width = grad.shape[1]
    mine = lax.dynamic_slice_in_dim(col_old, lax.axis_index("dp") * width, width)
    squares = grad * grad + tiny_value
    col_new = decay_rate * mine + (1.0 - decay_rate) * jnp.sum(squares, axis=0) / depth
    rowpart = jnp.sum(squares, axis=1)
    spent = jnp.sum(grad * grad * (1.0 / col_new)[None, :], axis=1)
    return rowpart, spent, col_new


def exchanged_step(normed, out_grad, w_up, w_down, row_up, col_up, row_down, col_down):
    n = lax.axis_size("dp")
    rows, width = w_up.shape[0], w_up.shape[1] // n
    depth = rows * n
    breadth = width * n * lax.axis_size("mp")
    normed_all, out_grad_all, cut_up, cut_down = spread(normed, out_grad, w_up, w_down)
    pre_act = jnp.dot(normed_all, cut_up, preferred_element_type=jnp.float32)
    act_value, pull_back = jax.vjp(gelu_tanh, pre_act)
    hidden_act = act_value.astype(jnp.bfloat16)
    act_grad = jnp.dot(out_grad_all, cut_down, preferred_element_type=jnp.float32)
    pre_grad = pull_back(act_grad)[0].astype(jnp.bfloat16)
    grad_down = lax.optimization_barrier(contract_tokens(out_grad_all, hidden_act))
    grad_up = lax.optimization_barrier(contract_tokens(normed_all, pre_grad))
    rowpart_up, spent_up, col_part_up = column_block(grad_up, col_up, depth)
    rowpart_down, spent_down, col_part_down = column_block(grad_down, col_down, depth)
    by_row = jnp.stack([rowpart_up, rowpart_down, spent_up, spent_down]).reshape(4, n, rows)
    by_col = jnp.broadcast_to(jnp.stack([col_part_up, col_part_down])[:, None], (2, n, width))
    stats = jnp.concatenate([by_row, by_col, jnp.zeros_like(by_col)]).transpose(1, 0, 2)
    moved_up, moved_down, gathered, row_new, energy = returned(
        grad_up.astype(jnp.bfloat16),
        grad_down.astype(jnp.bfloat16),
        stats,
        jnp.stack([row_up, row_down]),
        breadth,
    )
    col_new = gathered[:, 4:6].transpose(1, 0, 2).reshape(2, n * width)
    shrink = jnp.maximum(1.0, jnp.sqrt(energy[:, 0] / (depth * breadth)))
    update_up = finish_update(moved_up.astype(jnp.float32), row_new[0], col_new[0]) / shrink[0]
    update_down = finish_update(moved_down.astype(jnp.float32), row_new[1], col_new[1]) / shrink[1]
    return (update_up, update_down, row_new[0], col_new[0], row_new[1], col_new[1])


def on_device(
    token_pool,
    visible,
    out_grad,
    ln_gain,
    master_up,
    master_down,
    row_up,
    col_up,
    row_down,
    col_down,
):
    picked = jnp.take(token_pool, visible, axis=0).astype(jnp.float32)
    normed = normalize(picked, ln_gain)
    grid_rows = master_up.shape[0]
    grid_cols = master_up.shape[1]
    depth = grid_rows * lax.axis_size("dp")
    breadth = grid_cols * lax.axis_size("mp")
    w_up = master_up.astype(jnp.bfloat16)
    w_down = master_down.astype(jnp.bfloat16)
    if suits_exchange(master_up, normed):
        return exchanged_step(normed, out_grad, w_up, w_down, row_up, col_up, row_down, col_down)
    grad_up, grad_down = gathered_grads(normed, out_grad, w_up, w_down)
    squares_up = grad_up * grad_up + tiny_value
    squares_down = grad_down * grad_down + tiny_value
    rowpart_up = jnp.sum(squares_up, axis=1)
    rowpart_down = jnp.sum(squares_down, axis=1)
    colpart_up = jnp.sum(squares_up, axis=0)
    colpart_down = jnp.sum(squares_down, axis=0)
    rowsum_up, rowsum_down = lax.psum((rowpart_up, rowpart_down), "mp")
    colsum_up, colsum_down = lax.psum((colpart_up, colpart_down), "dp")
    row_up_new = decay_rate * row_up + (1.0 - decay_rate) * rowsum_up / breadth
    row_down_new = decay_rate * row_down + (1.0 - decay_rate) * rowsum_down / breadth
    col_up_new = decay_rate * col_up + (1.0 - decay_rate) * colsum_up / depth
    col_down_new = decay_rate * col_down + (1.0 - decay_rate) * colsum_down / depth
    raw_up = finish_update(grad_up, row_up_new, col_up_new)
    raw_down = finish_update(grad_down, row_down_new, col_down_new)
    energy_up, energy_down = lax.psum(
        (jnp.sum(raw_up * raw_up), jnp.sum(raw_down * raw_down)), ("dp", "mp")
    )
    update_up = raw_up / jnp.maximum(1.0, jnp.sqrt(energy_up / (depth * breadth)))
    update_down = raw_down / jnp.maximum(1.0, jnp.sqrt(energy_down / (depth * breadth)))
    return (update_up, update_down, row_up_new, col_up_new, row_down_new, col_down_new)


def solution(mesh):
    return jax.shard_map(
        on_device,
        mesh=mesh,
        in_specs=(
            P("dp", None),
            P("dp"),
            P("dp", None),
            P(),
            P("dp", "mp"),
            P("dp", "mp"),
            P("dp"),
            P("mp"),
            P("dp"),
            P("mp"),
        ),
        out_specs=(P("dp", "mp"), P("dp", "mp"), P("dp"), P("mp"), P("dp"), P("mp")),
        check_vma=False,
    )
```
